512 devices in a mesh: gz: 32 (over z_hi, x, y), gy: 16 (over z_lo, core).
Axes of the slice: x: 4, y: 4, z: 16 (z_hi: 2, z_lo: 8; z = z_hi * 8 + z_lo), core: 2. Of those that a mesh axis runs over, the one named last changes fastest.
Arguments:
- velocity: bfloat16 [3, 512, 256, 128], P(None, 'gz', 'gy'), may hold values from -6 to 6
- lag_table: int32 [5, 3], replicated, may hold values from -64 to 64, as said below
- filter_index: int32 [5, 16], replicated, may hold values from 0 to 31
- filter_weights: float32 [3, 32], replicated, may hold values from -4 to 4
Outputs:
- transfer: float32 [512, 256, 128], P('gz', 'gy')
The draws below stay inside these ranges and needn't reach their ends.
Inputs may be any that keep to these rules, and one draw needn't show every extreme that they name: `lag_table`: column 0 is a base x-offset from 0 to 48, column 1 a y lag from -4 to 4, column 2 a z lag from -64 to 64; one lag has z lag exactly 64 and another exactly -64.
All inputs are finite; a program needn't handle non-finite values.
Results may differ from the reference program's by a relative error of at most 0.0004.
Values may be sent and summed in bfloat16 or wider, within the bound.
No kernel may reach another device: no remote copies, remote signals or barrier semaphores. Data moves between devices by JAX's collectives and lax.ppermute only.
A program may use at most 64 MiB of HBM per device.

```python
import jax
import jax.numpy as jnp

NX = 128
NLAG = 5
NOFF = 16
REACH = 64
YREACH = 4
NW = 32
NZ = 512
NY = 256


def draw_lag_table(key, part):
    first = jax.random.randint(jax.random.fold_in(key, 11), (NLAG,), 0, 49)
    second = jax.random.randint(jax.random.fold_in(key, 12), (NLAG,), -YREACH, YREACH + 1)
    third = jax.random.randint(jax.random.fold_in(key, 13), (NLAG,), -REACH, REACH + 1)
    order = jax.random.permutation(jax.random.fold_in(key, 14), jnp.arange(NLAG, dtype=jnp.int32))
    slots = jnp.arange(NLAG, dtype=jnp.int32)
    third = jnp.where(slots == order[0], REACH, third)
    third = jnp.where(slots == order[1], -REACH, third)
    return jnp.stack([first, second, third], axis=1).astype(jnp.int32)


def place_ends(array, rng, least, largest):
    longest = array.shape.index(max(array.shape))
    spots = []
    for shift in (0, 1):
        where = [jax.random.randint(jax.random.fold_in(rng, axis), (), 0, length) for axis, length in enumerate(array.shape)]
        where[longest] = (where[longest] + shift) % array.shape[longest]
        spots.append(tuple(where))
    return array.at[spots[0]].set(least).at[spots[1]].set(largest)


def level_of(key, extent, shards, smallest, top_value):
    level = 1.0
    for dim, shards_of in shards:
        heights = jax.random.uniform(jax.random.fold_in(jax.random.fold_in(key, 6), dim), (shards_of,), jnp.float32, smallest / len(shards), top_value / len(shards))
        level = level * jnp.repeat(jnp.exp(heights), extent[dim] // shards_of).reshape((-1,) + (1,) * (len(extent) - 1 - dim))
    return level


def noise(key, shape, scale, reach, split=(), kind=jnp.bfloat16):
    gain = level_of(key, shape, split, -0.22, 0.18) if split else 1.0
    entries = jax.random.normal(key, shape, jnp.float32) * scale * gain
    return jnp.minimum(jnp.maximum(entries, -reach), reach).astype(kind)


def setup_inputs(seed: int = 0) -> dict:
    arg_keys = jax.random.split(jax.random.key(seed), 5)
    velocity = noise(arg_keys[0], (3, NZ, NY, NX), 1.0, 6.0, ((1, 32), (2, 16)))
    lag_table = draw_lag_table(jax.random.fold_in(arg_keys[4], 71), 0)
    filter_index = place_ends(jax.random.randint(arg_keys[2], (NLAG, NOFF), 0, NW), jax.random.fold_in(arg_keys[2], 1), 0, NW - 1).astype(jnp.int32)
    filter_weights = noise(arg_keys[3], (3, NW), 1.0, 4.0, (), jnp.float32)
    return {"velocity": velocity, "lag_table": lag_table, "filter_index": filter_index, "filter_weights": filter_weights}


def reference(velocity, lag_table, filter_index, filter_weights):
    field = velocity.astype(jnp.float32)
    total = jnp.zeros(field.shape[1:], jnp.float32)
    choices_index = jnp.arange(NW, dtype=jnp.int32)
    for lag in range(NLAG):
        base_x = lag_table[lag, 0]
        lag_y = lag_table[lag, 1]
        lag_z = lag_table[lag, 2]
        moved_yz = jnp.roll(field, (-lag_z, -lag_y), axis=(1, 2))
        for offset in range(NOFF):
            moved = jnp.roll(moved_yz, -(base_x + offset), axis=3)
            diff = moved - field
            pick = (choices_index == filter_index[lag, offset]).astype(jnp.float32)
            gradient = jnp.sum(filter_weights * pick[None, :], axis=1)
            along = gradient[0] * diff[0] + gradient[1] * diff[1] + gradient[2] * diff[2]
            energy = diff[0] * diff[0] + diff[1] * diff[1] + diff[2] * diff[2]
            total = total + along * energy
    return total * (0.25 / (NLAG * NOFF))
```

```python
import jax
import jax.numpy as jnp
from jax import lax
from jax.experimental import pallas as pl
from jax.experimental.pallas import tpu as pltpu
from jax.sharding import PartitionSpec as P

NLAG = 5
NOFF = 16
YREACH = 4
PLANES = 16
ROWS = 16
LANES = 128
AXES = ("gz", "gy")


def places():
    return [(h, x, y, g) for h in range(2) for x in range(4) for y in range(4) for g in range(16)]


def number(h, x, y, g):
    return ((h * 4 + x) * 4 + y) * 16 + g


def pairs(to):
    return [(number(*p), number(*to(*p))) for p in places()]


SWAP_A = pairs(lambda h, x, y, g: (h ^ (x % 3 == 0), 3 - x, y, g))
SWAP_B = pairs(lambda h, x, y, g: (h, x ^ 1, y, g))
SWAP_Y = [pairs(lambda h, x, y, g, k=k: (h, x, y ^ k, g)) for k in (1, 2, 3)]
SWAP_E = pairs(lambda h, x, y, g: (h, x, y, g ^ 1))
SWAP_O = pairs(lambda h, x, y, g: (h, x, y, (g + 1) % 16 if g % 2 else (g - 1) % 16))


def send(x, perm):
    return lax.ppermute(x, AXES, perm)


def sums_kernel(
    lag_ref, index_ref, weight_ref, u_ref, a_ref, b_ref, e_ref, o_ref, r1_ref, r2_ref, r3_ref,
    out_ref, field, base, gains,
):
    gz = lax.axis_index("gz")
    y = gz & 3
    odd_x = (gz >> 2) & 1
    odd_g = lax.axis_index("gy") & 1

    for block, ref in enumerate((u_ref, a_ref, b_ref)):
        for c in range(3):
            field[block, c, :, YREACH:YREACH + ROWS, :] = ref[c].astype(jnp.float32)
    for slot, ref in enumerate((u_ref, r1_ref, r2_ref, r3_ref)):
        base[slot] = ref[...].astype(jnp.float32)

    @pl.when(odd_g == 0)
    def _():
        field[:, :, :, 0:YREACH, :] = o_ref[...].astype(jnp.float32)
        field[:, :, :, YREACH + ROWS:, :] = e_ref[...].astype(jnp.float32)

    @pl.when(odd_g == 1)
    def _():
        field[:, :, :, 0:YREACH, :] = e_ref[...].astype(jnp.float32)
        field[:, :, :, YREACH + ROWS:, :] = o_ref[...].astype(jnp.float32)

    out_ref[...] = jnp.zeros_like(out_ref)

    def fill(n, carry):
        lag = n // NOFF
        k = n - lag * NOFF
        row = index_ref[lag, k]
        for c in range(3):
            gains[n, c] = jnp.full((8, LANES), weight_ref[c, row], jnp.float32)
        return carry

    lax.fori_loop(0, NLAG * NOFF, fill, 0)

    def step(n, carry):
        lag = n // PLANES
        plane = n - lag * PLANES
        start = lag_ref[lag, 0]
        lag_y = lag_ref[lag, 1]
        lag_z = lag_ref[lag, 2]
        whole = lag_z >> 4
        rest = lag_z & 15
        hops = whole + jnp.where(plane < rest, 1, 0)
        target = (y - hops) & 3
        column = (target + hops - y) >> 2
        block = jnp.where(column == 0, 0, jnp.where((column > 0) == (odd_x == 0), 2, 1))
        slot = y ^ target
        at = (plane - rest) & 15
        first = YREACH + lag_y
        moved = [
            [field[block, c, plane, pl.ds(first + 8 * half, 8), :] for c in range(3)]
            for half in range(2)
        ]
        here = [
            [base[slot, c, at, 8 * half:8 * half + 8, :] for c in range(3)] for half in range(2)
        ]
        sums = [out_ref[slot, at, 8 * half:8 * half + 8, :] for half in range(2)]
        for k in range(NOFF):
            shift = (2 * LANES - start - k) & (LANES - 1)
            g0, g1, g2 = (gains[lag * NOFF + k, c] for c in range(3))
            for half in range(2):
                d0, d1, d2 = (
                    pltpu.roll(moved[half][c], shift, 1) - here[half][c] for c in range(3)
                )
                along = g0 * d0 + g1 * d1 + g2 * d2
                energy = d0 * d0 + d1 * d1 + d2 * d2
                sums[half] = sums[half] + along * energy
        for half in range(2):
            out_ref[slot, at, 8 * half:8 * half + 8, :] = sums[half]
        return carry

    lax.fori_loop(0, NLAG * PLANES, step, 0)


def partial_sums(lag_table, filter_index, filter_weights, *fields):
    smem = pl.BlockSpec(memory_space=pltpu.SMEM)
    vmem = pl.BlockSpec(memory_space=pltpu.VMEM)
    return pl.pallas_call(
        sums_kernel,
        out_shape=jax.ShapeDtypeStruct((4, PLANES, ROWS, LANES), jnp.float32),
        in_specs=[smem] * 3 + [vmem] * len(fields),
        out_specs=vmem,
        scratch_shapes=[
            pltpu.VMEM((3, 3, PLANES, ROWS + 2 * YREACH, LANES), jnp.float32),
            pltpu.VMEM((4, 3, PLANES, ROWS, LANES), jnp.float32),
            pltpu.VMEM((NLAG * NOFF, 3, 8, LANES), jnp.float32),
        ],
        compiler_params=pltpu.CompilerParams(vmem_limit_bytes=16 << 20),
        name="sums",
    )(lag_table, filter_index, filter_weights, *fields)


def per_device(velocity, lag_table, filter_index, filter_weights):
    odd_g = lax.axis_index("gy") & 1
    a = send(velocity, SWAP_A)
    b = send(velocity, SWAP_B)
    r1, r2, r3 = (send(velocity, perm) for perm in SWAP_Y)
    blocks = jnp.stack([velocity, a, b])
    low = blocks[:, :, :, :YREACH]
    high = blocks[:, :, :, ROWS - YREACH:]
    e = send(jnp.where(odd_g == 0, high, low), SWAP_E)
    o = send(jnp.where(odd_g == 0, low, high), SWAP_O)
    sums = partial_sums(lag_table, filter_index, filter_weights, velocity, a, b, e, o, r1, r2, r3)
    p1, p2, p3 = (send(sums[k + 1], perm) for k, perm in enumerate(SWAP_Y))
    return (sums[0] + p1 + p2 + p3) * (0.25 / (NLAG * NOFF))


def solution(mesh):
    in_specs = (P(None, "gz", "gy", None), P(), P(), P())
    out_specs = P("gz", "gy", None)
    return jax.shard_map(
        per_device, mesh=mesh, in_specs=in_specs, out_specs=out_specs, check_vma=False
    )
```

```python
import jax
import jax.numpy as jnp
from jax import lax
from jax.experimental import pallas as pl
from jax.experimental.pallas import tpu as pltpu
from jax.sharding import Mesh
from jax.sharding import PartitionSpec as P


NLAG = 5
NOFF = 16
YREACH = 4
PLANES = 16
ROWS = 16
LANES = 128
AXES = ("zh", "x", "y", "zl", "c")
SIZES = (2, 4, 4, 8, 2)


def number(h, x, y, g):
    return ((h * 4 + x) * 4 + y) * 16 + g


def pairs(to):
    every = [(h, x, y, g) for h in range(2) for x in range(4) for y in range(4) for g in range(16)]
    return [(number(*p), number(*to(*p))) for p in every]


def beside(g):
    return (g + 1) % 16 if g % 2 else (g - 1) % 16


SWAP_A = pairs(lambda h, x, y, g: (h ^ (x % 3 == 0), 3 - x, y, g))
SWAP_B = pairs(lambda h, x, y, g: (h, x ^ 1, y, g))
SWAP_Y = [pairs(lambda h, x, y, g, k=k: (h, x, y ^ k, g)) for k in (1, 2, 3)]
SWAP_E = pairs(lambda h, x, y, g: (h, x, y, g ^ 1))
SWAP_O = pairs(lambda h, x, y, g: (h, x, y, beside(g)))
SWAP_AO = pairs(lambda h, x, y, g: (h ^ (x % 3 == 0), 3 - x, y, beside(g)))


def send(x, perm):
    return lax.ppermute(x, AXES, perm)


def put_main(field, block, main):
    field[block, :, :, YREACH:YREACH + ROWS, :] = main[...].astype(jnp.float32)


def put_halo(field, block, even, odd):
    c = lax.axis_index("c")

    @pl.when(c == 0)
    def _():
        field[block, :, :, 0:YREACH, :] = odd[...].astype(jnp.float32)
        field[block, :, :, YREACH + ROWS:, :] = even[...].astype(jnp.float32)

    @pl.when(c == 1)
    def _():
        field[block, :, :, 0:YREACH, :] = even[...].astype(jnp.float32)
        field[block, :, :, YREACH + ROWS:, :] = odd[...].astype(jnp.float32)


def list_planes(lag_ref, items, own):
    y = lax.axis_index("y")
    odd_x = lax.axis_index("x") & 1
    sink = (1 if own else 3) << 15
    items[0] = sink

    def segment(n, used):
        lag = n >> 1
        second = n & 1
        lag_z = lag_ref[lag, 2]
        rest = lag_z & (PLANES - 1)
        hops = (lag_z >> 4) + 1 - second
        low = jnp.where(second == 1, rest, 0)
        high = jnp.where(second == 1, PLANES, rest)
        target = (y - hops) & 3
        column = (target + hops - y) >> 2
        block = jnp.where(column == 0, 0, jnp.where((column > 0) == (odd_x == 1), 2, 1))
        slot = y ^ target
        high = jnp.where((slot == 0) == own, high, low)
        into = 0 if own else slot - 1
        fixed = (block << 4) | (lag << 6) | (into << 13) | (into << 15)

        def note(plane, used):
            items[used] = fixed | plane | (((plane - rest) & (PLANES - 1)) << 9)
            return used + 1

        return lax.fori_loop(low, high, note, used)

    used = lax.fori_loop(0, 2 * NLAG, segment, jnp.int32(1))
    for extra in range(3):
        items[used + extra] = sink
    return used - 1


def add_planes(lag_ref, field, base, gains, sums, items, turned0, turned1, parts0, parts1, own):
    count = list_planes(lag_ref, items, own)

    def turn(item, turned):
        plane = item & 15
        block = (item >> 4) & 3
        lag = (item >> 6) & 7
        at = (item >> 9) & 15
        slot = (item >> 13) & 3
        start = lag_ref[lag, 0]
        first = YREACH + lag_ref[lag, 1]
        for c in range(3):
            wide = base[slot, c, at].astype(jnp.float32)
            for h in range(2):
                moved = field[block, c, plane, pl.ds(first + 8 * h, 8), :]
                for i in range(4):
                    shift = (2 * LANES - start - 4 * i) & (LANES - 1)
                    turned[h, i, c] = pltpu.roll(moved, shift, 1)
                here = wide[8 * h:8 * h + 8]
                for j in range(4):
                    turned[h, 4 + j, c] = pltpu.roll(here, j, 1) if j else here

    def add(item, turned, parts):
        gain = ((item >> 6) & 7) * NOFF
        for h in range(2):
            for j in range(4):
                here = [turned[h, 4 + j, c] for c in range(3)]
                part = None
                for i in range(4):
                    g0, g1, g2 = (gains[gain + 4 * i + j, c] for c in range(3))
                    d0, d1, d2 = (turned[h, i, c] - here[c] for c in range(3))
                    along = g0 * d0 + g1 * d1 + g2 * d2
                    energy = d0 * d0 + d1 * d1 + d2 * d2
                    term = along * energy
                    part = term if part is None else part + term
                parts[h, j] = part

    def finish(item, parts):
        at = (item >> 9) & 15
        into = (item >> 15) & 3
        for h in range(2):
            total = sums[into, at, 8 * h:8 * h + 8, :] + parts[h, 0]
            for j in range(1, 4):
                total = total + pltpu.roll(parts[h, j], LANES - j, 1)
            sums[into, at, 8 * h:8 * h + 8, :] = total

    def two(i, carry):
        before, here, there, after = (items[2 * i + n] for n in range(4))
        add(here, turned0, parts0)
        turn(there, turned1)
        finish(before, parts1)
        add(there, turned1, parts1)
        turn(after, turned0)
        finish(here, parts0)
        return carry

    steps = (count + 1) >> 1
    parts1[...] = jnp.zeros_like(parts1)
    turn(items[1], turned0)
    lax.fori_loop(0, steps, two, 0)
    finish(items[2 * steps], parts1)


def prepare(index_ref, weight_ref, u_ref, b_ref, field, gains):
    def fill(lag, carry):
        for k in range(NOFF):
            row = index_ref[lag, k]
            for c in range(3):
                gains[lag * NOFF + k, c] = jnp.full((8, LANES), weight_ref[c, row], jnp.float32)
        return carry

    lax.fori_loop(0, NLAG, fill, 0)
    put_main(field, 0, u_ref)
    put_main(field, 1, b_ref)


def others(
    lag_ref, field_in, gains, a_ref, e_ref, o_ref, ao_ref, r1_ref, r2_ref, r3_ref,
    field, out1, out2, out3, base, sums, *work,
):
    del field_in
    put_main(field, 2, a_ref)
    put_halo(field, 0, e_ref.at[0], o_ref.at[0])
    put_halo(field, 1, e_ref.at[1], o_ref.at[1])
    put_halo(field, 2, e_ref.at[2], ao_ref)
    for slot, ref in enumerate((r1_ref, r2_ref, r3_ref)):
        base[slot] = ref[...]
    sums[...] = jnp.zeros_like(sums)
    add_planes(lag_ref, field, base, gains, sums, *work, False)
    for slot, ref in enumerate((out1, out2, out3)):
        ref[...] = sums[slot]


def selves(lag_ref, field, gains, u_ref, out, sums, *work):
    sums[...] = jnp.zeros_like(sums)
    add_planes(lag_ref, field, u_ref, gains, sums, *work, True)
    out[...] = sums[0]


WORK = [
    pltpu.SMEM((NLAG * PLANES + 4,), jnp.int32),
    pltpu.VMEM((2, 8, 3, 8, LANES), jnp.float32),
    pltpu.VMEM((2, 8, 3, 8, LANES), jnp.float32),
    pltpu.VMEM((2, 4, 8, LANES), jnp.float32),
    pltpu.VMEM((2, 4, 8, LANES), jnp.float32),
]
FIELD = jax.ShapeDtypeStruct((3, 3, PLANES, ROWS + 2 * YREACH, LANES), jnp.float32)
GAINS = jax.ShapeDtypeStruct((NLAG * NOFF, 3, 8, LANES), jnp.float32)
PART = jax.ShapeDtypeStruct((PLANES, ROWS, LANES), jnp.float32)


def call(kernel, scalars, fields, outs, flops, scratch=(), aliases=None):
    smem = pl.BlockSpec(memory_space=pltpu.SMEM)
    vmem = pl.BlockSpec(memory_space=pltpu.VMEM)
    return pl.pallas_call(
        kernel,
        out_shape=outs,
        in_specs=[smem] * len(scalars) + [vmem] * len(fields),
        out_specs=jax.tree.map(lambda _: vmem, outs),
        scratch_shapes=scratch,
        input_output_aliases=aliases or {},
        cost_estimate=pl.CostEstimate(flops=flops, bytes_accessed=4 << 20, transcendentals=0),
        compiler_params=pltpu.CompilerParams(vmem_limit_bytes=12 << 20),
    )(*scalars, *fields)


def per_device(velocity, lag_table, filter_index, filter_weights):
    c = lax.axis_index("c")

    def edge(x, upper):
        low = x[..., :YREACH, :]
        high = x[..., ROWS - YREACH:, :]
        return jnp.where(c == upper, high, low)

    a = send(velocity, SWAP_A)
    ao = send(edge(velocity, 1), SWAP_AO)
    b = send(velocity, SWAP_B)
    r1, r2, r3 = (send(velocity, perm) for perm in SWAP_Y)
    o = send(edge(jnp.stack([velocity, b]), 1), SWAP_O)
    field, gains = call(
        prepare, (filter_index, filter_weights), (velocity, b), (FIELD, GAINS), 1 << 21
    )
    trio = jnp.stack(lax.optimization_barrier((velocity, b, a)))
    e = send(edge(trio, 0), SWAP_E)
    field, s1, s2, s3 = call(
        others, (lag_table,), (field, gains, a, e, o, ao, r1, r2, r3),
        (FIELD, PART, PART, PART), 3 << 23,
        [pltpu.VMEM((3, 3, PLANES, ROWS, LANES), jnp.bfloat16),
         pltpu.VMEM((4, PLANES, ROWS, LANES), jnp.float32), *WORK], {1: 0},
    )
    p1, p2, p3 = (send(s, perm) for s, perm in zip((s1, s2, s3), SWAP_Y))
    own = call(
        selves, (lag_table,), (field, gains, velocity[None]), PART, 3 << 23,
        [pltpu.VMEM((2, PLANES, ROWS, LANES), jnp.float32), *WORK],
    )
    return (own + p1 + p2 + p3) * (0.25 / (NLAG * NOFF))


def solution(mesh):
    inner = Mesh(mesh.devices.reshape(SIZES), AXES)
    in_specs = (P(None, ("zh", "x", "y"), ("zl", "c"), None), P(), P(), P())
    out_specs = P(("zh", "x", "y"), ("zl", "c"), None)
    return jax.shard_map(
        per_device, mesh=inner, in_specs=in_specs, out_specs=out_specs, check_vma=False
    )
```

```python
import jax
import jax.numpy as jnp
from jax import lax
from jax.experimental import pallas as pl
from jax.experimental.pallas import tpu as pltpu
from jax.sharding import Mesh
from jax.sharding import PartitionSpec as P


NLAG = 5
NOFF = 16
YREACH = 4
PLANES = 16
ROWS = 16
LANES = 128
AXES = ("zh", "x", "y", "zl", "c")
SIZES = (2, 4, 4, 8, 2)


def number(h, x, y, g):
    return ((h * 4 + x) * 4 + y) * 16 + g


def pairs(to):
    every = [(h, x, y, g) for h in range(2) for x in range(4) for y in range(4) for g in range(16)]
    return [(number(*p), number(*to(*p))) for p in every]


def beside(g):
    return (g + 1) % 16 if g % 2 else (g - 1) % 16


SWAP_A = pairs(lambda h, x, y, g: (h ^ (x % 3 == 0), 3 - x, y, g))
SWAP_B = pairs(lambda h, x, y, g: (h, x ^ 1, y, g))
SWAP_Y = [pairs(lambda h, x, y, g, k=k: (h, x, y ^ k, g)) for k in (1, 2, 3)]
SWAP_E = pairs(lambda h, x, y, g: (h, x, y, g ^ 1))
SWAP_O = pairs(lambda h, x, y, g: (h, x, y, beside(g)))
SWAP_AO = pairs(lambda h, x, y, g: (h ^ (x % 3 == 0), 3 - x, y, beside(g)))


def send(x, perm):
    return lax.ppermute(x, AXES, perm)


def put_main(field, block, main):
    field[block, :, :, YREACH:YREACH + ROWS, :] = main[...].astype(jnp.float32)


def put_halo(field, block, even, odd):
    c = lax.axis_index("c")

    @pl.when(c == 0)
    def _():
        field[block, :, :, 0:YREACH, :] = odd[...].astype(jnp.float32)
        field[block, :, :, YREACH + ROWS:, :] = even[...].astype(jnp.float32)

    @pl.when(c == 1)
    def _():
        field[block, :, :, 0:YREACH, :] = even[...].astype(jnp.float32)
        field[block, :, :, YREACH + ROWS:, :] = odd[...].astype(jnp.float32)


def list_planes(lag_ref, items, own):
    y = lax.axis_index("y")
    odd_x = lax.axis_index("x") & 1
    sink = (1 if own else 3) << 15
    items[0] = sink

    def segment(n, used):
        lag = n >> 1
        second = n & 1
        lag_z = lag_ref[2, lag]
        rest = lag_z & (PLANES - 1)
        hops = (lag_z >> 4) + 1 - second
        low = jnp.where(second == 1, rest, 0)
        high = jnp.where(second == 1, PLANES, rest)
        target = (y - hops) & 3
        column = (target + hops - y) >> 2
        block = jnp.where(column == 0, 0, jnp.where((column > 0) == (odd_x == 1), 2, 1))
        slot = y ^ target
        high = jnp.where((slot == 0) == own, high, low)
        into = 0 if own else slot - 1
        fixed = (block << 4) | (lag << 6) | (into << 13) | (into << 15)

        def note(plane, used):
            items[used] = fixed | plane | (((plane - rest) & (PLANES - 1)) << 9)
            return used + 1

        return lax.fori_loop(low, high, note, used)

    used = lax.fori_loop(0, 2 * NLAG, segment, jnp.int32(1))
    for extra in range(3):
        items[used + extra] = sink
    return used - 1


def add_planes(lag_ref, field, base, gains, sums, items, turned0, turned1, parts0, parts1, own):
    count = list_planes(lag_ref, items, own)

    def turn(item, turned):
        plane = item & 15
        block = (item >> 4) & 3
        lag = (item >> 6) & 7
        at = (item >> 9) & 15
        slot = (item >> 13) & 3
        start = lag_ref[0, lag]
        first = YREACH + lag_ref[1, lag]
        for c in range(3):
            wide = base[slot, c, at].astype(jnp.float32)
            for h in range(2):
                moved = field[block, c, plane, pl.ds(first + 8 * h, 8), :]
                for i in range(4):
                    shift = (2 * LANES - start - 4 * i) & (LANES - 1)
                    turned[h, i, c] = pltpu.roll(moved, shift, 1)
                here = wide[8 * h:8 * h + 8]
                for j in range(4):
                    turned[h, 4 + j, c] = pltpu.roll(here, j, 1) if j else here

    def add(item, turned, parts):
        gain = ((item >> 6) & 7) * NOFF
        for h in range(2):
            for j in range(4):
                here = [turned[h, 4 + j, c] for c in range(3)]
                part = None
                for i in range(4):
                    g0, g1, g2 = (gains[gain + 4 * i + j, c] for c in range(3))
                    d0, d1, d2 = (turned[h, i, c] - here[c] for c in range(3))
                    along = g0 * d0 + g1 * d1 + g2 * d2
                    energy = d0 * d0 + d1 * d1 + d2 * d2
                    term = along * energy
                    part = term if part is None else part + term
                parts[h, j] = part

    def finish(item, parts):
        at = (item >> 9) & 15
        into = (item >> 15) & 3
        for h in range(2):
            total = sums[into, at, 8 * h:8 * h + 8, :] + parts[h, 0]
            for j in range(1, 4):
                total = total + pltpu.roll(parts[h, j], LANES - j, 1)
            sums[into, at, 8 * h:8 * h + 8, :] = total

    def two(i, carry):
        before, here, there, after = (items[2 * i + n] for n in range(4))
        add(here, turned0, parts0)
        turn(there, turned1)
        finish(before, parts1)
        add(there, turned1, parts1)
        turn(after, turned0)
        finish(here, parts0)
        return carry

    steps = (count + 1) >> 1
    parts1[...] = jnp.zeros_like(parts1)
    turn(items[1], turned0)
    lax.fori_loop(0, steps, two, 0)
    finish(items[2 * steps], parts1)


def pack(out, refs, upper):
    c = lax.axis_index("c")

    def take(first):
        for n, ref in enumerate(refs):
            for comp in range(3):
                half = ref[comp, :, 8 * (first // 8):8 * (first // 8) + 8, :].astype(jnp.float32)
                rows = half[:, first % 8:first % 8 + YREACH, :]
                out[n, comp] = rows.astype(jnp.bfloat16)

    pl.when(c == upper)(lambda: take(ROWS - YREACH))
    pl.when(c != upper)(lambda: take(0))


def first(u_hbm, u_ref, rows, sem):
    move = pltpu.make_async_copy(u_hbm, u_ref, sem)
    move.start()
    move.wait()
    pack(rows, (u_ref,), 1)


def pair(u_ref, r_ref, both):
    both[0] = u_ref[...]
    both[1] = r_ref[...]


def second(u_ref, b_ref, rows):
    pack(rows, (u_ref, b_ref), 1)


def third(u_ref, b_ref, a_ref, rows):
    pack(rows, (u_ref, b_ref, a_ref), 0)


def widen(index_ref, weight_ref, u_ref, b_ref, a_ref, field, gains):
    def fill(lag, carry):
        for k in range(NOFF):
            row = index_ref[lag, k]
            for c in range(3):
                gains[lag * NOFF + k, c] = jnp.full((8, LANES), weight_ref[c, row], jnp.float32)
        return carry

    lax.fori_loop(0, NLAG, fill, 0)
    for block, ref in enumerate((u_ref, b_ref, a_ref)):
        put_main(field, block, ref)


def others(
    lag_ref, field_in, gains, e_ref, o_ref, ao_ref, r_ref, both_ref,
    field, out1, out2, out3, base, sums, *work,
):
    del field_in
    put_halo(field, 0, e_ref.at[0], o_ref.at[0])
    put_halo(field, 1, e_ref.at[1], o_ref.at[1])
    put_halo(field, 2, e_ref.at[2], ao_ref.at[0])
    for slot, ref in enumerate((r_ref, both_ref.at[0], both_ref.at[1])):
        base[slot] = ref[...]
    sums[...] = jnp.zeros_like(sums)
    add_planes(lag_ref, field, base, gains, sums, *work, False)
    for slot, ref in enumerate((out1, out2, out3)):
        ref[...] = sums[slot]


def selves(lag_ref, field, gains, u_ref, out, sums, *work):
    sums[...] = jnp.zeros_like(sums)
    add_planes(lag_ref, field, u_ref, gains, sums, *work, True)
    out[...] = sums[0]


WORK = [
    pltpu.SMEM((NLAG * PLANES + 4,), jnp.int32),
    pltpu.VMEM((2, 8, 3, 8, LANES), jnp.float32),
    pltpu.VMEM((2, 8, 3, 8, LANES), jnp.float32),
    pltpu.VMEM((2, 4, 8, LANES), jnp.float32),
    pltpu.VMEM((2, 4, 8, LANES), jnp.float32),
]
FIELD = jax.ShapeDtypeStruct((3, 3, PLANES, ROWS + 2 * YREACH, LANES), jnp.float32)
BLOCK = jax.ShapeDtypeStruct((3, PLANES, ROWS, LANES), jnp.bfloat16)
GAINS = jax.ShapeDtypeStruct((NLAG * NOFF, 3, 8, LANES), jnp.float32)
PART = jax.ShapeDtypeStruct((PLANES, ROWS, LANES), jnp.float32)


def edges(blocks):
    return jax.ShapeDtypeStruct((blocks, 3, PLANES, YREACH, LANES), jnp.bfloat16)


def call(kernel, scalars, fields, outs, flops, scratch=(), aliases=None, space=pltpu.VMEM):
    smem = pl.BlockSpec(memory_space=pltpu.SMEM)
    vmem = pl.BlockSpec(memory_space=pltpu.VMEM)
    return pl.pallas_call(
        kernel,
        out_shape=outs,
        in_specs=[smem] * len(scalars) + [pl.BlockSpec(memory_space=space)] * len(fields),
        out_specs=jax.tree.map(lambda _: vmem, outs),
        scratch_shapes=scratch,
        input_output_aliases=aliases or {},
        cost_estimate=pl.CostEstimate(flops=flops, bytes_accessed=4 << 20, transcendentals=0),
        compiler_params=pltpu.CompilerParams(vmem_limit_bytes=12 << 20),
    )(*scalars, *fields)


def per_device(velocity, lag_table, filter_index, filter_weights):
    a = send(velocity, SWAP_A)
    b = send(velocity, SWAP_B)
    u, rows = call(
        first, (), (velocity,), (BLOCK, edges(1)), 1 << 20, [pltpu.SemaphoreType.DMA],
        space=pltpu.HBM,
    )
    ao = send(rows, SWAP_AO)
    r = send(velocity, SWAP_Y[0])
    both = jax.ShapeDtypeStruct((2, *BLOCK.shape), BLOCK.dtype)
    both = send(call(pair, (), (u, r), both, 1 << 20), SWAP_Y[1])
    o = send(call(second, (), (u, b), edges(2), 1 << 20), SWAP_O)
    e = send(call(third, (), (u, b, a), edges(3), 1 << 20), SWAP_E)
    field, gains = call(widen, (filter_index, filter_weights), (u, b, a), (FIELD, GAINS), 1 << 21)
    lags = lag_table.T
    field, s1, s2, s3 = call(
        others, (lags,), (field, gains, e, o, ao, r, both),
        (FIELD, PART, PART, PART), 3 << 23,
        [pltpu.VMEM((3, 3, PLANES, ROWS, LANES), jnp.bfloat16),
         pltpu.VMEM((4, PLANES, ROWS, LANES), jnp.float32), *WORK], {1: 0},
    )
    p1, p2, p3 = (send(s, perm) for s, perm in zip((s1, s2, s3), SWAP_Y))
    own = call(
        selves, (lags,), (field, gains, u[None]), PART, 3 << 23,
        [pltpu.VMEM((2, PLANES, ROWS, LANES), jnp.float32), *WORK],
    )
    return (own + p1 + p2 + p3) * (0.25 / (NLAG * NOFF))


def solution(mesh):
    inner = Mesh(mesh.devices.reshape(SIZES), AXES)
    in_specs = (P(None, ("zh", "x", "y"), ("zl", "c"), None), P(), P(), P())
    out_specs = P(("zh", "x", "y"), ("zl", "c"), None)
    return jax.shard_map(
        per_device, mesh=inner, in_specs=in_specs, out_specs=out_specs, check_vma=False
    )
```

```python
import jax
import jax.numpy as jnp
from jax import lax
from jax.experimental import pallas as pl
from jax.experimental.pallas import tpu as pltpu
from jax.sharding import Mesh
from jax.sharding import PartitionSpec as P


NLAG = 5
NOFF = 16
YREACH = 4
PLANES = 16
ROWS = 16
LANES = 128
AXES = ("zh", "x", "y", "zl", "c")
SIZES = (2, 4, 4, 8, 2)


def number(h, x, y, g):
    return ((h * 4 + x) * 4 + y) * 16 + g


def pairs(to, rows=range(16)):
    every = [(h, x, y, g) for h in range(2) for x in range(4) for y in range(4) for g in rows]
    return [(number(*p), number(*to(*p))) for p in every]


def beside(g):
    return (g + 1) % 16 if g % 2 else (g - 1) % 16


SWAP_A = pairs(lambda h, x, y, g: (h ^ (x % 3 == 0), 3 - x, y, g))
SWAP_B = pairs(lambda h, x, y, g: (h, x ^ 1, y, g))
SWAP_Y = [pairs(lambda h, x, y, g, k=k: (h, x, y ^ k, g)) for k in (1, 2, 3)]
SWAP_E = pairs(lambda h, x, y, g: (h, x, y, g ^ 1))
SWAP_O = pairs(lambda h, x, y, g: (h, x, y, beside(g)))
SWAP_AO = pairs(lambda h, x, y, g: (h ^ (x % 3 == 0), 3 - x, y, beside(g)), (0, 15))
SWAP_AN = pairs(lambda h, x, y, g: (h, x, y, beside(g)), range(1, 15))


def send(x, perm):
    return lax.ppermute(x, AXES, perm)


def put_main(field, block, main):
    field[block, :, :, YREACH:YREACH + ROWS, :] = main[...].astype(jnp.float32)


def put_halo(field, block, even, odd):
    c = lax.axis_index("c")

    @pl.when(c == 0)
    def _():
        field[block, :, :, 0:YREACH, :] = odd[...].astype(jnp.float32)
        field[block, :, :, YREACH + ROWS:, :] = even[...].astype(jnp.float32)

    @pl.when(c == 1)
    def _():
        field[block, :, :, 0:YREACH, :] = even[...].astype(jnp.float32)
        field[block, :, :, YREACH + ROWS:, :] = odd[...].astype(jnp.float32)


def list_planes(lag_ref, items, own):
    y = lax.axis_index("y")
    odd_x = lax.axis_index("x") & 1
    sink = (1 if own else 3) << 15
    items[0] = sink

    def segment(n, used):
        lag = n >> 1
        second = n & 1
        lag_z = lag_ref[2, lag]
        rest = lag_z & (PLANES - 1)
        hops = (lag_z >> 4) + 1 - second
        low = jnp.where(second == 1, rest, 0)
        high = jnp.where(second == 1, PLANES, rest)
        target = (y - hops) & 3
        column = (target + hops - y) >> 2
        block = jnp.where(column == 0, 0, jnp.where((column > 0) == (odd_x == 1), 2, 1))
        slot = y ^ target
        high = jnp.where((slot == 0) == own, high, low)
        into = 0 if own else slot - 1
        fixed = (block << 4) | (lag << 6) | (into << 13) | (into << 15)

        def note(plane, used):
            items[used] = fixed | plane | (((plane - rest) & (PLANES - 1)) << 9)
            return used + 1

        return lax.fori_loop(low, high, note, used)

    used = lax.fori_loop(0, 2 * NLAG, segment, jnp.int32(1))
    for extra in range(3):
        items[used + extra] = sink
    return used - 1


def add_planes(lag_ref, field, base, gains, sums, items, turned0, turned1, parts0, parts1, own):
    count = list_planes(lag_ref, items, own)

    def turn(item, turned):
        plane = item & 15
        block = (item >> 4) & 3
        lag = (item >> 6) & 7
        at = (item >> 9) & 15
        slot = (item >> 13) & 3
        start = lag_ref[0, lag]
        first = YREACH + lag_ref[1, lag]
        for c in range(3):
            wide = base[slot, c, at].astype(jnp.float32)
            for h in range(2):
                moved = field[block, c, plane, pl.ds(first + 8 * h, 8), :]
                for i in range(4):
                    shift = (2 * LANES - start - 4 * i) & (LANES - 1)
                    turned[h, i, c] = pltpu.roll(moved, shift, 1)
                here = wide[8 * h:8 * h + 8]
                for j in range(4):
                    turned[h, 4 + j, c] = pltpu.roll(here, j, 1) if j else here

    def add(item, turned, parts):
        gain = ((item >> 6) & 7) * NOFF
        for h in range(2):
            for j in range(4):
                here = [turned[h, 4 + j, c] for c in range(3)]
                part = None
                for i in range(4):
                    g0, g1, g2 = (gains[gain + 4 * i + j, c] for c in range(3))
                    d0, d1, d2 = (turned[h, i, c] - here[c] for c in range(3))
                    along = g0 * d0 + g1 * d1 + g2 * d2
                    energy = d0 * d0 + d1 * d1 + d2 * d2
                    term = along * energy
                    part = term if part is None else part + term
                parts[h, j] = part

    def finish(item, parts):
        at = (item >> 9) & 15
        into = (item >> 15) & 3
        for h in range(2):
            total = sums[into, at, 8 * h:8 * h + 8, :] + parts[h, 0]
            for j in range(1, 4):
                total = total + pltpu.roll(parts[h, j], LANES - j, 1)
            sums[into, at, 8 * h:8 * h + 8, :] = total

    def two(i, carry):
        before, here, there, after = (items[2 * i + n] for n in range(4))
        add(here, turned0, parts0)
        turn(there, turned1)
        finish(before, parts1)
        add(there, turned1, parts1)
        turn(after, turned0)
        finish(here, parts0)
        return carry

    steps = (count + 1) >> 1
    parts1[...] = jnp.zeros_like(parts1)
    turn(items[1], turned0)
    lax.fori_loop(0, steps, two, 0)
    finish(items[2 * steps], parts1)


def pack(out, refs, upper):
    c = lax.axis_index("c")

    def take(first):
        for n, ref in enumerate(refs):
            for comp in range(3):
                half = ref[comp, :, 8 * (first // 8):8 * (first // 8) + 8, :].astype(jnp.float32)
                rows = half[:, first % 8:first % 8 + YREACH, :]
                out[n, comp] = rows.astype(jnp.bfloat16)

    pl.when(c == upper)(lambda: take(ROWS - YREACH))
    pl.when(c != upper)(lambda: take(0))


def first(u_hbm, u_ref, rows, sem):
    move = pltpu.make_async_copy(u_hbm, u_ref, sem)
    move.start()
    move.wait()
    pack(rows, (u_ref,), 1)


def pair(u_ref, r_ref, both):
    both[0] = u_ref[...]
    both[1] = r_ref[...]


def second(u_ref, b_ref, rows):
    pack(rows, (u_ref, b_ref), 1)


def third(u_ref, b_ref, a_ref, rows, beside_rows):
    pack(beside_rows, (a_ref,), 1)
    pack(rows, (u_ref, b_ref, a_ref), 0)


def widen(index_ref, weight_ref, u_ref, b_ref, a_ref, field, gains):
    def fill(lag, carry):
        for k in range(NOFF):
            row = index_ref[lag, k]
            for c in range(3):
                gains[lag * NOFF + k, c] = jnp.full((8, LANES), weight_ref[c, row], jnp.float32)
        return carry

    lax.fori_loop(0, NLAG, fill, 0)
    for block, ref in enumerate((u_ref, b_ref, a_ref)):
        put_main(field, block, ref)


def others(
    lag_ref, field_in, gains, e_ref, o_ref, ao_ref, an_ref, r_ref, both_ref,
    field, out1, out2, out3, base, sums, *work,
):
    del field_in
    put_halo(field, 0, e_ref.at[0], o_ref.at[0])
    put_halo(field, 1, e_ref.at[1], o_ref.at[1])
    put_halo(field, 2, e_ref.at[2], ao_ref[0].astype(jnp.float32) + an_ref[0].astype(jnp.float32))
    for slot, ref in enumerate((r_ref, both_ref.at[0], both_ref.at[1])):
        base[slot] = ref[...]
    sums[...] = jnp.zeros_like(sums)
    add_planes(lag_ref, field, base, gains, sums, *work, False)
    for slot, ref in enumerate((out1, out2, out3)):
        ref[...] = sums[slot]


def selves(lag_ref, field, gains, u_ref, out, sums, *work):
    sums[...] = jnp.zeros_like(sums)
    add_planes(lag_ref, field, u_ref, gains, sums, *work, True)
    out[...] = sums[0]


WORK = [
    pltpu.SMEM((NLAG * PLANES + 4,), jnp.int32),
    pltpu.VMEM((2, 8, 3, 8, LANES), jnp.float32),
    pltpu.VMEM((2, 8, 3, 8, LANES), jnp.float32),
    pltpu.VMEM((2, 4, 8, LANES), jnp.float32),
    pltpu.VMEM((2, 4, 8, LANES), jnp.float32),
]
FIELD = jax.ShapeDtypeStruct((3, 3, PLANES, ROWS + 2 * YREACH, LANES), jnp.float32)
BLOCK = jax.ShapeDtypeStruct((3, PLANES, ROWS, LANES), jnp.bfloat16)
GAINS = jax.ShapeDtypeStruct((NLAG * NOFF, 3, 8, LANES), jnp.float32)
PART = jax.ShapeDtypeStruct((PLANES, ROWS, LANES), jnp.float32)


def edges(blocks):
    return jax.ShapeDtypeStruct((blocks, 3, PLANES, YREACH, LANES), jnp.bfloat16)


def call(kernel, scalars, fields, outs, flops, scratch=(), aliases=None, space=pltpu.VMEM):
    smem = pl.BlockSpec(memory_space=pltpu.SMEM)
    vmem = pl.BlockSpec(memory_space=pltpu.VMEM)
    return pl.pallas_call(
        kernel,
        out_shape=outs,
        in_specs=[smem] * len(scalars) + [pl.BlockSpec(memory_space=space)] * len(fields),
        out_specs=jax.tree.map(lambda _: vmem, outs),
        scratch_shapes=scratch,
        input_output_aliases=aliases or {},
        cost_estimate=pl.CostEstimate(flops=flops, bytes_accessed=4 << 20, transcendentals=0),
        compiler_params=pltpu.CompilerParams(vmem_limit_bytes=12 << 20),
    )(*scalars, *fields)


def per_device(velocity, lag_table, filter_index, filter_weights):
    a = send(velocity, SWAP_A)
    b = send(velocity, SWAP_B)
    u, rows = call(
        first, (), (velocity,), (BLOCK, edges(1)), 1 << 20, [pltpu.SemaphoreType.DMA],
        space=pltpu.HBM,
    )
    ao = send(rows, SWAP_AO)
    r = send(velocity, SWAP_Y[0])
    both = jax.ShapeDtypeStruct((2, *BLOCK.shape), BLOCK.dtype)
    both = send(call(pair, (), (u, r), both, 1 << 20), SWAP_Y[1])
    o = send(call(second, (), (u, b), edges(2), 1 << 20), SWAP_O)
    rows, beside_rows = call(third, (), (u, b, a), (edges(3), edges(1)), 1 << 20)
    an = send(beside_rows, SWAP_AN)
    e = send(rows, SWAP_E)
    field, gains = call(widen, (filter_index, filter_weights), (u, b, a), (FIELD, GAINS), 1 << 21)
    lags = lag_table.T
    field, s1, s2, s3 = call(
        others, (lags,), (field, gains, e, o, ao, an, r, both),
        (FIELD, PART, PART, PART), 3 << 23,
        [pltpu.VMEM((3, 3, PLANES, ROWS, LANES), jnp.bfloat16),
         pltpu.VMEM((4, PLANES, ROWS, LANES), jnp.float32), *WORK], {1: 0},
    )
    p1, p2, p3 = (send(s, perm) for s, perm in zip((s1, s2, s3), SWAP_Y))
    own = call(
        selves, (lags,), (field, gains, u[None]), PART, 3 << 23,
        [pltpu.VMEM((2, PLANES, ROWS, LANES), jnp.float32), *WORK],
    )
    return (own + p1 + p2 + p3) * (0.25 / (NLAG * NOFF))


def solution(mesh):
    inner = Mesh(mesh.devices.reshape(SIZES), AXES)
    in_specs = (P(None, ("zh", "x", "y"), ("zl", "c"), None), P(), P(), P())
    out_specs = P(("zh", "x", "y"), ("zl", "c"), None)
    return jax.shard_map(
        per_device, mesh=inner, in_specs=in_specs, out_specs=out_specs, check_vma=False
    )
```
